32 devices in a mesh: order: 8 (over z, x), chan: 4 (over y, core).
Axes of the slice: x: 2, y: 2, z: 4, core: 2. Of those that a mesh axis runs over, the one named last changes fastest.
Arguments:
- cotangent: bfloat16 [248, 240, 1, 2, 1024], P('order', None, None, None, 'chan'), may hold values from -0.59765625 to 0.59765625
- stored_coefficients: bfloat16 [248, 240, 1, 2, 1024], P('order', None, None, None, 'chan'), may hold values from -0.29882812 to 0.29882812
- weights: bfloat16 [248, 1024, 1024], P('order', 'chan'), may hold values from -0.1875 to 0.1875
- order_table: int32 [248], replicated, may hold values from 0 to 240, as said below
- degree_table: int32 [248], replicated, may hold values from 0 to 240, as said below
Outputs:
- input_gradient: bfloat16 [248, 240, 1, 2, 1024], P('order', None, None, None, 'chan')
- mixing_gradient: bfloat16 [248, 1024, 1024], P('order', 'chan')
The draws below stay inside these ranges and needn't reach their ends.
Inputs may be any that keep to these rules, and one draw needn't show every extreme that they name: `order_table`: each order 0 to 239 stands in exactly one slot; every other slot holds 240, meaning empty. `degree_table`: each degree 0 to 239 stands in exactly one slot; every other slot holds 240, meaning empty.
All inputs are finite; a program needn't handle non-finite values.
Results may differ from the reference program's by a relative error of at most 0.008.
Values may be sent and summed in bfloat16 or wider, within the bound.
A program may use at most 192 MiB of HBM per device.

```python
import jax
import jax.numpy as jnp
from jax import lax

DEGREE_COUNT = 240
LATITUDE_COUNT = 240
CHANNEL_COUNT = 1024
BATCH_SAMPLES = 1
TOTAL_SLOTS = 248


def draw_order_table(key, part):
    permuted_values = jax.random.permutation(jax.random.fold_in(key, 101), TOTAL_SLOTS)
    return jnp.minimum(permuted_values, DEGREE_COUNT).astype(jnp.int32)


def draw_degree_table(key, part):
    permuted_values = jax.random.permutation(jax.random.fold_in(key, 202), TOTAL_SLOTS)
    return jnp.minimum(permuted_values, DEGREE_COUNT).astype(jnp.int32)


def levels(stream_key, extent, split, least, largest):
    def one(position, shards_of):
        draws = jax.random.uniform(jax.random.fold_in(jax.random.fold_in(stream_key, 6), position), (shards_of,), jnp.float32, least / len(split), largest / len(split))
        return jnp.repeat(jnp.exp(draws), extent[position] // shards_of).reshape((-1,) + (1,) * (len(extent) - position - 1))

    loudness = one(*split[0])
    for cut in split[1:]:
        loudness = loudness * one(*cut)
    return loudness


def noise(key, dims, deviation, bound, pieces=(), held_as=jnp.bfloat16):
    values = jax.random.normal(key, dims, jnp.float32) * deviation
    if len(pieces) > 0:
        values = levels(key, dims, pieces, -0.22, 0.18) * values
    return jnp.clip(values, min=-bound, max=bound).astype(held_as)


def setup_inputs(seed: int = 0) -> dict:
    keys = jax.random.split(jax.random.key(seed), 6)
    return {
        "cotangent": noise(keys[0], (TOTAL_SLOTS, LATITUDE_COUNT, BATCH_SAMPLES, 2, CHANNEL_COUNT), 0.1, 0.59765625, ((0, 8), (4, 4))),
        "stored_coefficients": noise(keys[1], (TOTAL_SLOTS, DEGREE_COUNT, BATCH_SAMPLES, 2, CHANNEL_COUNT), 0.05, 0.29882812, ((0, 8), (4, 4))),
        "weights": noise(keys[2], (TOTAL_SLOTS, CHANNEL_COUNT, CHANNEL_COUNT), CHANNEL_COUNT ** -0.5, 0.1875, ((0, 8), (1, 4))),
        "order_table": draw_order_table(jax.random.fold_in(keys[5], 71), 0),
        "degree_table": draw_degree_table(jax.random.fold_in(keys[5], 71), 0),
    }


def legendre_rows(orders, degree_range, latitude_count):
    order_real = orders.astype(jnp.float32)[:, None]
    angles = jnp.pi * (jnp.arange(latitude_count).astype(jnp.float32) + 0.5) / latitude_count
    cosine = jnp.cos(angles)[None, :]
    sine = jnp.sin(angles)[None, :]
    counter = jnp.arange(1, degree_range + 1).astype(jnp.float32)
    factors = jnp.log((2.0 * counter - 1.0) / (2.0 * counter))
    below = (counter[None, :] <= order_real).astype(jnp.float32)
    log_start = 0.5 * (jnp.log((2.0 * order_real + 1.0) / (4.0 * jnp.pi)) + lax.optimization_barrier(jnp.sum(below * factors[None, :], axis=1, keepdims=True)))
    parity = 1.0 - 2.0 * (orders % 2).astype(jnp.float32)[:, None]
    start = parity * jnp.exp(log_start + order_real * jnp.log(sine))

    def advance(carry, degree):
        latest, before = carry
        level = degree.astype(jnp.float32)
        upper = jnp.sqrt(jnp.maximum(4.0 * level * level - 1.0, 0.0) / jnp.maximum(level * level - order_real * order_real, 1.0))
        lower = jnp.sqrt(jnp.maximum((level - 1.0) * (level - 1.0) - order_real * order_real, 0.0) / jnp.maximum(4.0 * (level - 1.0) * (level - 1.0) - 1.0, 1.0))
        grown = upper * (cosine * latest - lower * before)
        fresh = jnp.where(level == order_real, start, jnp.where(level > order_real, grown, jnp.zeros_like(grown)))
        return ((fresh, latest), fresh)
    zeros = jnp.zeros((orders.shape[0], latitude_count), jnp.float32)
    unused_result, stacked = lax.scan(advance, (zeros, zeros), jnp.arange(degree_range).astype(jnp.int32))
    return jnp.transpose(stacked, (1, 0, 2))

def quadrature(latitude_count):
    angles = jnp.pi * (jnp.arange(latitude_count).astype(jnp.float32) + 0.5) / latitude_count
    return jnp.pi / latitude_count * jnp.sin(angles)

def reference(cotangent, stored_coefficients, weights, order_table, degree_table):
    slot_count, latitude_count, batch_size, unused_result, slot_width = cotangent.shape
    degree_range = stored_coefficients.shape[1]
    feature_count = batch_size * 2 * slot_width
    table = legendre_rows(order_table, degree_range, latitude_count)
    table_halfprecision = table.astype(jnp.bfloat16)
    flat_cotangent = cotangent.reshape(slot_count, latitude_count, feature_count)

    def synth_adjoint(items):
        table_one, cot_one = items
        return jnp.dot(table_one.astype(jnp.float32), cot_one.astype(jnp.float32), preferred_element_type=jnp.float32).astype(jnp.bfloat16)
    adjoint = lax.map(synth_adjoint, (table_halfprecision, flat_cotangent))
    active_mask = jnp.arange(degree_range).astype(jnp.int32)[None, :] >= order_table[:, None]
    masked_values = stored_coefficients.reshape(slot_count, degree_range, feature_count) * active_mask[:, :, None].astype(jnp.bfloat16)
    clipped = jnp.minimum(degree_table, degree_range - 1).astype(jnp.int32)
    valid_degree = degree_table < degree_range

    def per_degree(items):
        degree_one, valid_one, weight_one = items
        left_row_block = lax.dynamic_index_in_dim(masked_values, degree_one, 1, keepdims=False)
        right_row_block = lax.dynamic_index_in_dim(adjoint, degree_one, 1, keepdims=False)
        left_flattened = left_row_block.reshape(slot_count * batch_size * 2, slot_width).astype(jnp.float32)
        right_flattened = right_row_block.reshape(slot_count * batch_size * 2, slot_width).astype(jnp.float32)
        weight_gradient = jnp.dot(left_flattened.T, right_flattened, preferred_element_type=jnp.float32)
        weight_gradient = jnp.where(valid_one, weight_gradient, jnp.zeros_like(weight_gradient)).astype(jnp.bfloat16)
        coefficient_gradient = jnp.dot(right_flattened, weight_one.astype(jnp.float32).T, preferred_element_type=jnp.float32)
        coefficient_gradient = jnp.where(valid_one, coefficient_gradient, jnp.zeros_like(coefficient_gradient)).astype(jnp.bfloat16)
        return (weight_gradient, coefficient_gradient.reshape(slot_count, feature_count))
    mixing_gradient, grad_coeff = lax.map(per_degree, (clipped, valid_degree, weights))
    quad = quadrature(latitude_count)

    def order_values(items):
        table_one, index_one = items
        picked = jnp.take(table_one, clipped, axis=0) * valid_degree[:, None].astype(jnp.bfloat16)
        grads = lax.dynamic_index_in_dim(grad_coeff, index_one, 1, keepdims=False)
        summed = jnp.dot(picked.astype(jnp.float32).T, grads.astype(jnp.float32), preferred_element_type=jnp.float32)
        return (summed * quad[:, None]).astype(jnp.bfloat16)
    input_gradient = lax.map(order_values, (table_halfprecision, jnp.arange(slot_count).astype(jnp.int32)))
    return (input_gradient.reshape(slot_count, latitude_count, batch_size, 2, slot_width), mixing_gradient)
```

```python
import functools

import jax
import jax.numpy as jnp
from jax import lax
from jax.experimental import pallas as pl
from jax.experimental.pallas import tpu as pltpu
from jax.sharding import PartitionSpec as P


SPREADS = (1.85, 2.55, 3.3)
VMEM_LIMIT = 60 * 1024 * 1024
LANES = 128


def recurrence_kernel(unroll, where_ref, upper_ref, lower_ref, order_ref, cosine_ref, start_ref, out_ref):
    degree_range = upper_ref.shape[0]
    latitude_count = out_ref.shape[2]
    pieces = [(lo, min(lo + LANES, latitude_count)) for lo in range(0, latitude_count, LANES)]
    out_ref[...] = jnp.zeros_like(out_ref)
    order = order_ref[...]
    cosine = [cosine_ref[:, lo:hi] for lo, hi in pieces]
    start = [start_ref[:, lo:hi] for lo, hi in pieces]

    def body(step, carry):
        latest, before = carry
        for inner in range(unroll):
            level = step * unroll + inner
            row = where_ref[level]
            upper = upper_ref[level]
            lower = lower_ref[level]
            begins = order == level
            fresh = []
            for i, (lo, hi) in enumerate(pieces):
                width = hi - lo
                grown = upper[:, :width] * (cosine[i] * latest[i] - lower[:, :width] * before[i])
                value = jnp.where(begins[:, :width], start[i], grown)
                out_ref[row, :, lo:hi] = value.astype(jnp.bfloat16)
                fresh.append(value)
            latest, before = fresh, latest
        return latest, before

    zeros = [jnp.zeros_like(c) for c in cosine]
    lax.fori_loop(0, degree_range // unroll, body, (zeros, zeros))


def picked_legendre(orders, degree_table, degree_range, latitude_count):
    slots = orders.shape[0]
    total = degree_table.shape[0]
    order_real = orders.astype(jnp.float32)[:, None]
    angles = jnp.pi * (jnp.arange(latitude_count).astype(jnp.float32) + 0.5) / latitude_count
    cosine = jnp.cos(angles)[None, :]
    sine = jnp.sin(angles)[None, :]
    counter = jnp.arange(1, degree_range + 1).astype(jnp.float32)
    factors = jnp.log((2.0 * counter - 1.0) / (2.0 * counter))
    below = (counter[None, :] <= order_real).astype(jnp.float32)
    log_start = 0.5 * (
        jnp.log((2.0 * order_real + 1.0) / (4.0 * jnp.pi))
        + jnp.sum(below * factors[None, :], axis=1, keepdims=True)
    )
    parity = 1.0 - 2.0 * (orders % 2).astype(jnp.float32)[:, None]
    start = parity * jnp.exp(log_start + order_real * jnp.log(sine))

    level = jnp.arange(degree_range).astype(jnp.float32)[:, None]
    order_wide = order_real[:, 0][None, :]
    upper = jnp.sqrt(
        jnp.maximum(4.0 * level * level - 1.0, 0.0)
        / jnp.maximum(level * level - order_wide * order_wide, 1.0)
    )
    lower = jnp.sqrt(
        jnp.maximum((level - 1.0) * (level - 1.0) - order_wide * order_wide, 0.0)
        / jnp.maximum(4.0 * (level - 1.0) * (level - 1.0) - 1.0, 1.0)
    )
    upper, lower = (
        jnp.broadcast_to(lax.optimization_barrier(part)[:, :, None], part.shape + (LANES,))
        for part in (upper, lower)
    )
    places = jnp.arange(total).astype(jnp.int32)
    degrees = jnp.arange(degree_range).astype(jnp.int32)
    where = jnp.sum(
        jnp.where(degree_table[None, :] == degrees[:, None], places[None, :], 0), axis=1
    )
    where = jnp.minimum(where, total - 1).astype(jnp.int32)
    unroll = next(u for u in (8, 6, 5, 4, 3, 2, 1) if degree_range % u == 0)
    vmem = pl.BlockSpec(memory_space=pltpu.VMEM)
    return pl.pallas_call(
        functools.partial(recurrence_kernel, unroll),
        out_shape=jax.ShapeDtypeStruct((total, slots, latitude_count), jnp.bfloat16),
        in_specs=[pl.BlockSpec(memory_space=pltpu.SMEM)] + [vmem] * 5,
        out_specs=vmem,
        cost_estimate=pl.CostEstimate(
            flops=6 * degree_range * slots * latitude_count,
            bytes_accessed=24 * 1024 * 1024,
            transcendentals=0,
        ),
        name="legendre",
    )(
        where,
        upper,
        lower,
        jnp.broadcast_to(orders[:, None], (slots, LANES)),
        jnp.broadcast_to(cosine, (slots, latitude_count)),
        start,
    )


def quadrature(latitude_count):
    angles = jnp.pi * (jnp.arange(latitude_count).astype(jnp.float32) + 0.5) / latitude_count
    return jnp.pi / latitude_count * jnp.sin(angles)


def exchange(value):
    return lax.all_to_all(value, "order", split_axis=0, concat_axis=0, tiled=True)


def pack(packer, value):
    return jnp.einsum(
        "tpks,tksc->tpc", packer, value, preferred_element_type=jnp.float32
    ).astype(jnp.bfloat16)


def swap(value, bit):
    count = lax.axis_size("chan")
    return lax.ppermute(value, "chan", [(i, i ^ bit) for i in range(count)])


def gather_channels(value):
    count = lax.axis_size("chan")
    if count & (count - 1):
        whole = lax.all_gather(value, "chan", axis=0)
        return [whole[i] for i in range(count)], jnp.arange(count).astype(jnp.int32)
    blocks, flips = [value], [0]
    bit = count // 2
    while bit:
        blocks = blocks + [swap(block, bit) for block in blocks]
        flips = flips + [flip ^ bit for flip in flips]
        bit //= 2
    owners = jnp.bitwise_xor(lax.axis_index("chan"), jnp.array(flips, jnp.int32))
    return blocks, owners


def window_rows(plan_ref, peers, step, window):
    base = step * peers * 3
    spans = []
    for p in range(peers):
        where = pl.multiple_of(plan_ref[base + 3 * p], 16)
        spans.append((pl.ds(where, window), plan_ref[base + 3 * p + 1], plan_ref[base + 3 * p + 2]))
    return spans


def coefficient_kernel(peers, window, blocks, plan_ref, owner_ref, *refs):
    gathered, (weight_ref, out_ref) = refs[:blocks], refs[blocks:]
    step = pl.program_id(0)
    width = out_ref.shape[2]

    @pl.when(step == 0)
    def _():
        out_ref[...] = jnp.zeros_like(out_ref)

    spans = window_rows(plan_ref, peers, step, window)
    total = None
    for b, ref in enumerate(gathered):
        rows = jnp.concatenate([ref[p, span, :] for p, (span, _, _) in enumerate(spans)], axis=0)
        lanes = pl.ds(pl.multiple_of(owner_ref[b] * width, width), width)
        part = lax.dot_general(
            rows, weight_ref[0, :, lanes], (((1,), (1,)), ((), ())), preferred_element_type=jnp.float32
        )
        total = part if total is None else total + part
    index = lax.broadcasted_iota(jnp.int32, (window, width), 0)
    for p, (span, first, _) in enumerate(spans):
        kept = out_ref[p, span, :].astype(jnp.float32)
        fresh = total[p * window : (p + 1) * window]
        out_ref[p, span, :] = jnp.where(index >= first, fresh, kept).astype(jnp.bfloat16)


def mixing_kernel(peers, window, blocks, rows_of, plan_ref, owner_ref, *refs):
    gathered = [refs[r * blocks : (r + 1) * blocks] for r in range(rows_of)]
    saved = refs[rows_of * blocks : rows_of * (blocks + 1)]
    out_ref = refs[-1]
    step = pl.program_id(0)
    width = saved[0].shape[2]
    spans = window_rows(plan_ref, peers, step, window)
    index = lax.broadcasted_iota(jnp.int32, (window, width), 0)
    masked = []
    for r in range(rows_of):
        for p, (span, first, last) in enumerate(spans):
            value = saved[r][p, span, :].astype(jnp.float32)
            inside = (index >= first) & (index < last)
            masked.append(jnp.where(inside, value, 0.0).astype(jnp.bfloat16))
    left = jnp.concatenate(masked, axis=0)
    for b in range(blocks):
        right = jnp.concatenate(
            [gathered[r][b][p, span, :] for r in range(rows_of) for p, (span, _, _) in enumerate(spans)],
            axis=0,
        )
        lanes = pl.ds(pl.multiple_of(owner_ref[b] * width, width), width)
        out_ref[0, :, lanes] = lax.dot_general(
            left, right, (((0,), (0,)), ((), ())), preferred_element_type=jnp.float32
        ).astype(jnp.bfloat16)


def whole_block(shape):
    return pl.BlockSpec(shape, lambda k, *_: (0,) * len(shape), pipeline_mode=pl.Buffered(1))


def coefficients(plan, owners, window, gathered, weights):
    slots, width, channels = weights.shape
    peers = gathered[0].shape[0]
    kernel = functools.partial(coefficient_kernel, peers, window, len(gathered))
    return pl.pallas_call(
        kernel,
        grid_spec=pltpu.PrefetchScalarGridSpec(
            num_scalar_prefetch=2,
            grid=(slots,),
            in_specs=[whole_block(part.shape) for part in gathered]
            + [pl.BlockSpec((1, width, channels), lambda k, *_: (k, 0, 0))],
            out_specs=whole_block(gathered[0].shape),
        ),
        out_shape=jax.ShapeDtypeStruct(gathered[0].shape, jnp.bfloat16),
        compiler_params=pltpu.CompilerParams(vmem_limit_bytes=VMEM_LIMIT),
        cost_estimate=pl.CostEstimate(
            flops=2 * slots * peers * window * width * channels,
            bytes_accessed=2 * (weights.size + (len(gathered) + 1) * gathered[0].size),
            transcendentals=0,
        ),
        name="coefficients",
    )(plan, owners, *gathered, weights)


def mixing_gradients(plan, owners, window, gathered, saved, slots):
    rows_of, blocks = len(gathered), len(gathered[0])
    peers, _, width = saved[0].shape
    operands = [part for parts in gathered for part in parts] + list(saved)
    return pl.pallas_call(
        functools.partial(mixing_kernel, peers, window, blocks, rows_of),
        grid_spec=pltpu.PrefetchScalarGridSpec(
            num_scalar_prefetch=2,
            grid=(slots,),
            in_specs=[whole_block(part.shape) for part in operands],
            out_specs=pl.BlockSpec((1, width, width * blocks), lambda k, *_: (k, 0, 0)),
        ),
        out_shape=jax.ShapeDtypeStruct((slots, width, width * blocks), jnp.bfloat16),
        compiler_params=pltpu.CompilerParams(vmem_limit_bytes=VMEM_LIMIT),
        cost_estimate=pl.CostEstimate(
            flops=2 * slots * peers * window * rows_of * width * width * blocks,
            bytes_accessed=2 * (slots * width * width * blocks + len(operands) * saved[0].size),
            transcendentals=0,
        ),
        name="mixing",
    )(plan, owners, *operands)


def layer(capacity, *operands):
    return layer_body(capacity, *operands)


def layer_body(
    capacity, cotangent, stored_coefficients, weights, order_table, degree_table, mine, owned
):
    slots, latitude_count, batch_size, parts, width = cotangent.shape
    degree_range = stored_coefficients.shape[1]
    peers = lax.axis_size("order")
    full = slots * slots
    rows = batch_size * parts
    cot = cotangent.reshape(slots, latitude_count, rows, width)
    stored = stored_coefficients.reshape(slots, degree_range, rows, width)
    degrees = jnp.arange(degree_range).astype(jnp.int32)

    valid = (degree_table[:, None] >= mine[None, :]) & (degree_table[:, None] < degree_range)
    flags = valid.reshape(peers, full).astype(jnp.bfloat16)
    index = jnp.arange(full)
    before = (index[:, None] < index[None, :]).astype(jnp.bfloat16)
    rank = jnp.dot(flags, before, preferred_element_type=jnp.float32).astype(jnp.int32)
    rank = jnp.where(valid.reshape(peers, full), rank, -1).reshape(peers, slots, slots)
    place = jnp.arange(capacity).astype(jnp.int32)[None, :, None, None]
    packer = (rank[:, None] == place).astype(jnp.bfloat16)

    window = min(-(-slots // 16) * 16 + 16, capacity)
    lengths = jnp.sum(
        (
            (order_table.reshape(peers, slots)[None] <= owned[:, None, None])
            & (owned[:, None, None] < degree_range)
        ).astype(jnp.int32),
        axis=2,
    )
    steps = jnp.arange(slots)
    earlier = (steps[:, None] > steps[None, :]).astype(jnp.int32)
    offsets = jnp.sum(earlier[:, :, None] * lengths[None], axis=1)
    starts = jnp.minimum(offsets // 16 * 16, capacity - window)
    first = offsets - starts
    plan = jnp.stack([starts, first, first + lengths], axis=2).reshape(-1).astype(jnp.int32)

    pick = (degree_table[:, None, None] == degrees[None, None, :]) & valid[:, :, None]
    pick = pick.astype(jnp.bfloat16).reshape(peers, slots, slots, degree_range)

    def project(matrix, source):
        return jnp.einsum(
            "tksj,sjc->tksc", matrix, source, preferred_element_type=jnp.float32
        ).astype(jnp.bfloat16)

    def send_saved(r):
        return exchange(pack(packer, project(pick, stored[:, :, r])))

    def send_adjoint(r):
        moved = exchange(pack(packer, project(table, cot[:, :, r])))
        return gather_channels(moved)

    saved = [send_saved(0)]
    table = picked_legendre(mine, degree_table, degree_range, latitude_count)
    table = table.reshape(peers, slots, slots, latitude_count)
    gathered = []
    for r in range(rows):
        blocks, owners = send_adjoint(r)
        gathered.append(blocks)
    saved += [send_saved(r) for r in range(1, rows)]
    quad = quadrature(latitude_count)
    outputs = []
    for r in range(rows):
        coefficient = coefficients(plan, owners, window, gathered[r], weights)
        moved = exchange(coefficient)
        returned = jnp.einsum(
            "tpks,tpc->tksc", packer, moved, preferred_element_type=jnp.float32
        ).astype(jnp.bfloat16)
        summed = jnp.einsum("tksj,tksc->sjc", table, returned, preferred_element_type=jnp.float32)
        outputs.append((summed * quad[None, :, None]).astype(jnp.bfloat16))
    mixing_gradient = mixing_gradients(plan, owners, window, gathered, saved, slots)
    return jnp.stack(outputs, axis=2).reshape(cotangent.shape), mixing_gradient


def capacities(slots, peers, degree_range):
    full = slots * slots
    live = degree_range * (degree_range + 1) / 2 / (peers * slots) ** 2
    spread = (full * (2 * slots + 1) / 12) ** 0.5
    most = -(-full // 16) * 16
    steps = [-(-int(live * full + s * spread) // 16) * 16 for s in SPREADS]
    return [c for c in steps if c <= 0.85 * most] + [most]


def per_device(cotangent, stored_coefficients, weights, order_table, degree_table):
    slots = cotangent.shape[0]
    degree_range = stored_coefficients.shape[1]
    peers = lax.axis_size("order")
    position = lax.axis_index("order")
    mine = lax.dynamic_slice_in_dim(order_table, position * slots, slots)
    owned = lax.dynamic_slice_in_dim(degree_table, position * slots, slots)
    operands = (cotangent, stored_coefficients, weights, order_table, degree_table, mine, owned)
    tiers = capacities(slots, peers, degree_range)
    if len(tiers) == 1:
        return layer_body(tiers[0], *operands)
    order_rows = order_table.reshape(peers, 1, slots, 1)
    degree_rows = degree_table.reshape(1, peers, 1, slots)
    counts = jnp.sum(
        ((degree_rows >= order_rows) & (degree_rows < degree_range)).astype(jnp.int32), axis=(2, 3)
    )
    most = jnp.max(counts)
    tier = sum((most > c).astype(jnp.int32) for c in tiers[:-1])
    return lax.switch(tier, [functools.partial(layer, c) for c in tiers], *operands)


def solution(mesh):
    return jax.shard_map(
        per_device,
        mesh=mesh,
        in_specs=(
            P("order", None, None, None, "chan"),
            P("order", None, None, None, "chan"),
            P("order", "chan", None),
            P(),
            P(),
        ),
        out_specs=(P("order", None, None, None, "chan"), P("order", "chan", None)),
        check_vma=False,
    )
```

```python
import functools

import jax
import jax.numpy as jnp
from jax import lax
from jax.experimental import pallas as pl
from jax.experimental.pallas import tpu as pltpu
from jax.sharding import PartitionSpec as P


SPREADS = (2.1, 2.8, 3.5)
VMEM_LIMIT = 60 * 1024 * 1024
LANES = 128


def recurrence_kernel(unroll, where_ref, upper_ref, lower_ref, order_ref, cosine_ref, start_ref, out_ref):
    degree_range = upper_ref.shape[0]
    latitude_count = out_ref.shape[2]
    pieces = [(lo, min(lo + LANES, latitude_count)) for lo in range(0, latitude_count, LANES)]
    out_ref[...] = jnp.zeros_like(out_ref)
    order = order_ref[...]
    cosine = [cosine_ref[:, lo:hi] for lo, hi in pieces]
    start = [start_ref[:, lo:hi] for lo, hi in pieces]

    def body(step, carry):
        latest, before = carry
        for inner in range(unroll):
            level = step * unroll + inner
            row = where_ref[level]
            upper = upper_ref[level]
            lower = lower_ref[level]
            begins = order == level
            fresh = []
            for i, (lo, hi) in enumerate(pieces):
                width = hi - lo
                grown = upper[:, :width] * (cosine[i] * latest[i] - lower[:, :width] * before[i])
                value = jnp.where(begins[:, :width], start[i], grown)
                out_ref[row, :, lo:hi] = value.astype(jnp.bfloat16)
                fresh.append(value)
            latest, before = fresh, latest
        return latest, before

    zeros = [jnp.zeros_like(c) for c in cosine]
    lax.fori_loop(0, degree_range // unroll, body, (zeros, zeros))


def picked_legendre(orders, degree_table, degree_range, latitude_count):
    slots = orders.shape[0]
    total = degree_table.shape[0]
    order_real = orders.astype(jnp.float32)[:, None]
    angles = jnp.pi * (jnp.arange(latitude_count).astype(jnp.float32) + 0.5) / latitude_count
    cosine = jnp.cos(angles)[None, :]
    sine = jnp.sin(angles)[None, :]
    counter = jnp.arange(1, degree_range + 1).astype(jnp.float32)
    factors = jnp.log((2.0 * counter - 1.0) / (2.0 * counter))
    below = (counter[None, :] <= order_real).astype(jnp.float32)
    log_start = 0.5 * (
        jnp.log((2.0 * order_real + 1.0) / (4.0 * jnp.pi))
        + jnp.sum(below * factors[None, :], axis=1, keepdims=True)
    )
    parity = 1.0 - 2.0 * (orders % 2).astype(jnp.float32)[:, None]
    start = parity * jnp.exp(log_start + order_real * jnp.log(sine))

    level = jnp.arange(degree_range).astype(jnp.float32)[:, None]
    order_wide = order_real[:, 0][None, :]
    upper = jnp.sqrt(
        jnp.maximum(4.0 * level * level - 1.0, 0.0)
        / jnp.maximum(level * level - order_wide * order_wide, 1.0)
    )
    lower = jnp.sqrt(
        jnp.maximum((level - 1.0) * (level - 1.0) - order_wide * order_wide, 0.0)
        / jnp.maximum(4.0 * (level - 1.0) * (level - 1.0) - 1.0, 1.0)
    )
    upper, lower = (
        jnp.broadcast_to(lax.optimization_barrier(part)[:, :, None], part.shape + (LANES,))
        for part in (upper, lower)
    )
    places = jnp.arange(total).astype(jnp.int32)
    degrees = jnp.arange(degree_range).astype(jnp.int32)
    where = jnp.sum(
        jnp.where(degree_table[None, :] == degrees[:, None], places[None, :], 0), axis=1
    )
    where = jnp.minimum(where, total - 1).astype(jnp.int32)
    unroll = next(u for u in (8, 6, 5, 4, 3, 2, 1) if degree_range % u == 0)
    vmem = pl.BlockSpec(memory_space=pltpu.VMEM)
    return pl.pallas_call(
        functools.partial(recurrence_kernel, unroll),
        out_shape=jax.ShapeDtypeStruct((total, slots, latitude_count), jnp.bfloat16),
        in_specs=[pl.BlockSpec(memory_space=pltpu.SMEM)] + [vmem] * 5,
        out_specs=vmem,
        cost_estimate=pl.CostEstimate(
            flops=6 * degree_range * slots * latitude_count,
            bytes_accessed=24 * 1024 * 1024,
            transcendentals=0,
        ),
        name="legendre",
    )(
        where,
        upper,
        lower,
        jnp.broadcast_to(orders[:, None], (slots, LANES)),
        jnp.broadcast_to(cosine, (slots, latitude_count)),
        start,
    )


def quadrature(latitude_count):
    angles = jnp.pi * (jnp.arange(latitude_count).astype(jnp.float32) + 0.5) / latitude_count
    return jnp.pi / latitude_count * jnp.sin(angles)


def exchange(value):
    return lax.all_to_all(value, "order", split_axis=0, concat_axis=0, tiled=True)


def pack(packer, value):
    return jnp.einsum(
        "tpks,tksc->tpc", packer, value, preferred_element_type=jnp.float32
    ).astype(jnp.bfloat16)


def final_kernel(others, table_ref, value_ref, quad_ref, *refs):
    earlier, out_ref = refs[:others], refs[others]
    batch, count = table_ref.shape[:2]
    for i in range(batch):
        values = value_ref[i].reshape(count, value_ref.shape[-1])
        summed = lax.dot_general(
            table_ref[i], values, (((0,), (0,)), ((), ())), preferred_element_type=jnp.float32
        )
        parts = [ref[i].astype(jnp.float32) for ref in earlier] + [summed * quad_ref[...]]
        out_ref[i] = jnp.stack(parts, axis=1).astype(jnp.bfloat16)


def final_rows(table, values, quad, earlier):
    slots, count, latitude_count = table.shape
    peers, padded, width = values.shape[1:]
    batch = min(4, slots)
    parts = len(earlier) + 1
    return pl.pallas_call(
        functools.partial(final_kernel, len(earlier)),
        grid=(-(-slots // batch),),
        in_specs=[
            pl.BlockSpec((batch, count, latitude_count), lambda i: (i, 0, 0)),
            pl.BlockSpec((batch, peers, padded, width), lambda i: (i, 0, 0, 0)),
            pl.BlockSpec(quad.shape, lambda i: (0, 0)),
        ]
        + [pl.BlockSpec((batch, latitude_count, width), lambda i: (i, 0, 0))] * len(earlier),
        out_specs=pl.BlockSpec((batch, latitude_count, parts, width), lambda i: (i, 0, 0, 0)),
        out_shape=jax.ShapeDtypeStruct((slots, latitude_count, parts, width), jnp.bfloat16),
        compiler_params=pltpu.CompilerParams(vmem_limit_bytes=VMEM_LIMIT),
        cost_estimate=pl.CostEstimate(
            flops=2 * table.size * width,
            bytes_accessed=2 * (table.size + values.size + 2 * parts * slots * latitude_count * width),
            transcendentals=0,
        ),
        name="final",
    )(table, values, quad, *earlier)


def swap(value, bit):
    count = lax.axis_size("chan")
    return lax.ppermute(value, "chan", [(i, i ^ bit) for i in range(count)])


def gather_channels(value):
    count = lax.axis_size("chan")
    if count & (count - 1):
        whole = lax.all_gather(value, "chan", axis=0)
        return [whole[i] for i in range(count)], jnp.arange(count).astype(jnp.int32)
    blocks, flips = [value], [0]
    bit = count // 2
    while bit:
        blocks = blocks + [swap(block, bit) for block in blocks]
        flips = flips + [flip ^ bit for flip in flips]
        bit //= 2
    owners = jnp.bitwise_xor(lax.axis_index("chan"), jnp.array(flips, jnp.int32))
    return blocks, owners


def window_rows(plan_ref, peers, step, window):
    base = step * peers * 3
    spans = []
    for p in range(peers):
        where = pl.multiple_of(plan_ref[base + 3 * p], 16)
        spans.append((pl.ds(where, window), plan_ref[base + 3 * p + 1], plan_ref[base + 3 * p + 2]))
    return spans


def coefficient_kernel(peers, window, blocks, plan_ref, owner_ref, *refs):
    gathered, (weight_ref, out_ref) = refs[:blocks], refs[blocks:]
    step = pl.program_id(0)
    width = out_ref.shape[2]

    @pl.when(step == 0)
    def _():
        out_ref[...] = jnp.zeros_like(out_ref)

    spans = window_rows(plan_ref, peers, step, window)
    total = None
    for b, ref in enumerate(gathered):
        rows = jnp.concatenate([ref[p, span, :] for p, (span, _, _) in enumerate(spans)], axis=0)
        lanes = pl.ds(pl.multiple_of(owner_ref[b] * width, width), width)
        part = lax.dot_general(
            rows, weight_ref[0, :, lanes], (((1,), (1,)), ((), ())), preferred_element_type=jnp.float32
        )
        total = part if total is None else total + part
    index = lax.broadcasted_iota(jnp.int32, (window, width), 0)
    for p, (span, first, _) in enumerate(spans):
        kept = out_ref[p, span, :].astype(jnp.float32)
        fresh = total[p * window : (p + 1) * window]
        out_ref[p, span, :] = jnp.where(index >= first, fresh, kept).astype(jnp.bfloat16)


def mixing_kernel(peers, window, blocks, rows_of, plan_ref, owner_ref, *refs):
    gathered = [refs[r * blocks : (r + 1) * blocks] for r in range(rows_of)]
    saved = refs[rows_of * blocks : rows_of * (blocks + 1)]
    out_ref = refs[-1]
    step = pl.program_id(0)
    width = saved[0].shape[2]
    spans = window_rows(plan_ref, peers, step, window)
    index = lax.broadcasted_iota(jnp.int32, (window, width), 0)
    masked = []
    for r in range(rows_of):
        for p, (span, first, last) in enumerate(spans):
            value = saved[r][p, span, :].astype(jnp.float32)
            inside = (index >= first) & (index < last)
            masked.append(jnp.where(inside, value, 0.0).astype(jnp.bfloat16))
    left = jnp.concatenate(masked, axis=0)
    for b in range(blocks):
        right = jnp.concatenate(
            [gathered[r][b][p, span, :] for r in range(rows_of) for p, (span, _, _) in enumerate(spans)],
            axis=0,
        )
        lanes = pl.ds(pl.multiple_of(owner_ref[b] * width, width), width)
        out_ref[0, :, lanes] = lax.dot_general(
            left, right, (((0,), (0,)), ((), ())), preferred_element_type=jnp.float32
        ).astype(jnp.bfloat16)


def whole_block(shape):
    return pl.BlockSpec(shape, lambda k, *_: (0,) * len(shape), pipeline_mode=pl.Buffered(1))


def coefficients(plan, owners, window, gathered, weights):
    slots, width, channels = weights.shape
    peers = gathered[0].shape[0]
    kernel = functools.partial(coefficient_kernel, peers, window, len(gathered))
    return pl.pallas_call(
        kernel,
        grid_spec=pltpu.PrefetchScalarGridSpec(
            num_scalar_prefetch=2,
            grid=(slots,),
            in_specs=[whole_block(part.shape) for part in gathered]
            + [pl.BlockSpec((1, width, channels), lambda k, *_: (k, 0, 0))],
            out_specs=whole_block(gathered[0].shape),
        ),
        out_shape=jax.ShapeDtypeStruct(gathered[0].shape, jnp.bfloat16),
        compiler_params=pltpu.CompilerParams(vmem_limit_bytes=VMEM_LIMIT),
        cost_estimate=pl.CostEstimate(
            flops=2 * slots * peers * window * width * channels,
            bytes_accessed=2 * (weights.size + (len(gathered) + 1) * gathered[0].size),
            transcendentals=0,
        ),
        name="coefficients",
    )(plan, owners, *gathered, weights)


def mixing_gradients(plan, owners, window, gathered, saved, slots):
    rows_of, blocks = len(gathered), len(gathered[0])
    peers, _, width = saved[0].shape
    operands = [part for parts in gathered for part in parts] + list(saved)
    return pl.pallas_call(
        functools.partial(mixing_kernel, peers, window, blocks, rows_of),
        grid_spec=pltpu.PrefetchScalarGridSpec(
            num_scalar_prefetch=2,
            grid=(slots,),
            in_specs=[whole_block(part.shape) for part in operands],
            out_specs=pl.BlockSpec((1, width, width * blocks), lambda k, *_: (k, 0, 0)),
        ),
        out_shape=jax.ShapeDtypeStruct((slots, width, width * blocks), jnp.bfloat16),
        compiler_params=pltpu.CompilerParams(vmem_limit_bytes=VMEM_LIMIT),
        cost_estimate=pl.CostEstimate(
            flops=2 * slots * peers * window * rows_of * width * width * blocks,
            bytes_accessed=2 * (slots * width * width * blocks + len(operands) * saved[0].size),
            transcendentals=0,
        ),
        name="mixing",
    )(plan, owners, *operands)


def layer(capacity, *operands):
    return layer_body(capacity, *operands)


def layer_body(
    capacity, cotangent, stored_coefficients, weights, order_table, degree_table, mine, owned
):
    slots, latitude_count, batch_size, parts, width = cotangent.shape
    degree_range = stored_coefficients.shape[1]
    peers = lax.axis_size("order")
    full = slots * slots
    rows = batch_size * parts
    cot = cotangent.reshape(slots, latitude_count, rows, width)
    stored = stored_coefficients.reshape(slots, degree_range, rows, width)
    degrees = jnp.arange(degree_range).astype(jnp.int32)

    valid = (degree_table[:, None] >= mine[None, :]) & (degree_table[:, None] < degree_range)
    flags = valid.reshape(peers, full).astype(jnp.bfloat16)
    index = jnp.arange(full)
    before = (index[:, None] < index[None, :]).astype(jnp.bfloat16)
    rank = jnp.dot(flags, before, preferred_element_type=jnp.float32).astype(jnp.int32)
    rank = jnp.where(valid.reshape(peers, full), rank, -1).reshape(peers, slots, slots)
    place = jnp.arange(capacity).astype(jnp.int32)[None, :, None, None]
    packer = (rank[:, None] == place).astype(jnp.bfloat16)

    padded = -(-slots // 16) * 16
    spare = padded - slots
    wide = jnp.pad(rank, ((0, 0), (0, spare), (0, 0)), constant_values=-1)
    wide_packer = (wide[:, None] == place).astype(jnp.bfloat16)

    window = min(-(-slots // 16) * 16 + 16, capacity)
    lengths = jnp.sum(
        (
            (order_table.reshape(peers, slots)[None] <= owned[:, None, None])
            & (owned[:, None, None] < degree_range)
        ).astype(jnp.int32),
        axis=2,
    )
    steps = jnp.arange(slots)
    earlier = (steps[:, None] > steps[None, :]).astype(jnp.int32)
    offsets = jnp.sum(earlier[:, :, None] * lengths[None], axis=1)
    starts = jnp.minimum(offsets // 16 * 16, capacity - window)
    first = offsets - starts
    plan = jnp.stack([starts, first, first + lengths], axis=2).reshape(-1).astype(jnp.int32)

    pick = (degree_table[:, None, None] == degrees[None, None, :]) & valid[:, :, None]
    pick = pick.astype(jnp.bfloat16).reshape(peers, slots, slots, degree_range)

    def project(matrix, source):
        return jnp.einsum(
            "tksj,sjc->tksc", matrix, source, preferred_element_type=jnp.float32
        ).astype(jnp.bfloat16)

    def send_saved(r):
        return exchange(pack(packer, project(pick, stored[:, :, r])))

    def send_adjoint(r):
        moved = exchange(pack(packer, project(table, cot[:, :, r])))
        return gather_channels(moved)

    saved = [send_saved(0)]
    table = picked_legendre(mine, degree_table, degree_range, latitude_count)
    table = table.reshape(peers, slots, slots, latitude_count)
    turned = jnp.pad(table, ((0, 0), (0, spare), (0, 0), (0, 0))).transpose(2, 0, 1, 3)
    turned = turned.reshape(slots, peers * padded, latitude_count)
    gathered = []
    for r in range(rows):
        blocks, owners = send_adjoint(r)
        gathered.append(blocks)
    saved += [send_saved(r) for r in range(1, rows)]
    quad = quadrature(latitude_count)
    outputs = []
    for r in range(rows):
        coefficient = coefficients(plan, owners, window, gathered[r], weights)
        moved = exchange(coefficient)
        form = "tpks,tpc->tksc" if r < rows - 1 else "tpks,tpc->stkc"
        returned = jnp.einsum(
            form,
            packer if r < rows - 1 else wide_packer,
            moved,
            preferred_element_type=jnp.float32,
        ).astype(jnp.bfloat16)
        if r < rows - 1:
            summed = jnp.einsum(
                "tksj,tksc->sjc", table, returned, preferred_element_type=jnp.float32
            )
            outputs.append((summed * quad[None, :, None]).astype(jnp.bfloat16))
        else:
            spread = jnp.broadcast_to(quad[:, None], (latitude_count, width))
            outputs = final_rows(turned, returned, spread, outputs)
    mixing_gradient = mixing_gradients(plan, owners, window, gathered, saved, slots)
    return outputs.reshape(cotangent.shape), mixing_gradient


def capacities(slots, peers, degree_range):
    full = slots * slots
    live = degree_range * (degree_range + 1) / 2 / (peers * slots) ** 2
    spread = (full * (2 * slots + 1) / 12) ** 0.5
    most = -(-full // 16) * 16
    steps = [-(-int(live * full + s * spread) // 16) * 16 for s in SPREADS]
    return [c for c in steps if c <= 0.85 * most] + [most]


def choose(tier, tiers, operands):
    first = functools.partial(layer, tiers[0])
    if len(tiers) == 1:
        return first(*operands)
    return lax.cond(tier == 0, first, lambda *rest: choose(tier - 1, tiers[1:], rest), *operands)


def per_device(cotangent, stored_coefficients, weights, order_table, degree_table):
    slots = cotangent.shape[0]
    degree_range = stored_coefficients.shape[1]
    peers = lax.axis_size("order")
    position = lax.axis_index("order")
    mine = lax.dynamic_slice_in_dim(order_table, position * slots, slots)
    owned = lax.dynamic_slice_in_dim(degree_table, position * slots, slots)
    operands = (cotangent, stored_coefficients, weights, order_table, degree_table, mine, owned)
    tiers = capacities(slots, peers, degree_range)
    if len(tiers) == 1:
        return layer_body(tiers[0], *operands)
    order_rows = order_table.reshape(peers, 1, slots, 1)
    degree_rows = degree_table.reshape(1, peers, 1, slots)
    counts = jnp.sum(
        ((degree_rows >= order_rows) & (degree_rows < degree_range)).astype(jnp.int32), axis=(2, 3)
    )
    most = jnp.max(counts)
    tier = sum((most > c).astype(jnp.int32) for c in tiers[:-1])
    return choose(tier, tiers, operands)


def solution(mesh):
    return jax.shard_map(
        per_device,
        mesh=mesh,
        in_specs=(
            P("order", None, None, None, "chan"),
            P("order", None, None, None, "chan"),
            P("order", "chan", None),
            P(),
            P(),
        ),
        out_specs=(P("order", None, None, None, "chan"), P("order", "chan", None)),
        check_vma=False,
    )
```

```python
import functools

import jax
import jax.numpy as jnp
from jax import lax
from jax.experimental import pallas as pl
from jax.experimental.pallas import tpu as pltpu
from jax.sharding import PartitionSpec as P


SPREADS = (2.1, 2.8, 3.5)
VMEM_LIMIT = 60 * 1024 * 1024
LANES = 128


def recurrence_kernel(unroll, where_ref, upper_ref, lower_ref, order_ref, cosine_ref, start_ref, out_ref):
    degree_range = upper_ref.shape[0]
    latitude_count = out_ref.shape[2]
    pieces = [(lo, min(lo + LANES, latitude_count)) for lo in range(0, latitude_count, LANES)]
    out_ref[...] = jnp.zeros_like(out_ref)
    order = order_ref[...]
    cosine = [cosine_ref[:, lo:hi] for lo, hi in pieces]
    start = [start_ref[:, lo:hi] for lo, hi in pieces]

    def body(step, carry):
        latest, before = carry
        for inner in range(unroll):
            level = step * unroll + inner
            row = where_ref[level]
            upper = upper_ref[level]
            lower = lower_ref[level]
            begins = order == level
            fresh = []
            for i, (lo, hi) in enumerate(pieces):
                width = hi - lo
                grown = upper[:, :width] * (cosine[i] * latest[i] - lower[:, :width] * before[i])
                value = jnp.where(begins[:, :width], start[i], grown)
                out_ref[row, :, lo:hi] = value.astype(jnp.bfloat16)
                fresh.append(value)
            latest, before = fresh, latest
        return latest, before

    zeros = [jnp.zeros_like(c) for c in cosine]
    lax.fori_loop(0, degree_range // unroll, body, (zeros, zeros))


def picked_legendre(orders, degree_table, degree_range, latitude_count):
    slots = orders.shape[0]
    total = degree_table.shape[0]
    order_real = orders.astype(jnp.float32)[:, None]
    angles = jnp.pi * (jnp.arange(latitude_count).astype(jnp.float32) + 0.5) / latitude_count
    cosine = jnp.cos(angles)[None, :]
    sine = jnp.sin(angles)[None, :]
    counter = jnp.arange(1, degree_range + 1).astype(jnp.float32)
    factors = jnp.log((2.0 * counter - 1.0) / (2.0 * counter))
    below = (counter[None, :] <= order_real).astype(jnp.float32)
    log_start = 0.5 * (
        jnp.log((2.0 * order_real + 1.0) / (4.0 * jnp.pi))
        + jnp.sum(below * factors[None, :], axis=1, keepdims=True)
    )
    parity = 1.0 - 2.0 * (orders % 2).astype(jnp.float32)[:, None]
    start = parity * jnp.exp(log_start + order_real * jnp.log(sine))

    level = jnp.arange(degree_range).astype(jnp.float32)[:, None]
    order_wide = order_real[:, 0][None, :]
    upper = jnp.sqrt(
        jnp.maximum(4.0 * level * level - 1.0, 0.0)
        / jnp.maximum(level * level - order_wide * order_wide, 1.0)
    )
    lower = jnp.sqrt(
        jnp.maximum((level - 1.0) * (level - 1.0) - order_wide * order_wide, 0.0)
        / jnp.maximum(4.0 * (level - 1.0) * (level - 1.0) - 1.0, 1.0)
    )
    upper, lower = (
        jnp.broadcast_to(lax.optimization_barrier(part)[:, :, None], part.shape + (LANES,))
        for part in (upper, lower)
    )
    places = jnp.arange(total).astype(jnp.int32)
    degrees = jnp.arange(degree_range).astype(jnp.int32)
    where = jnp.sum(
        jnp.where(degree_table[None, :] == degrees[:, None], places[None, :], 0), axis=1
    )
    where = jnp.minimum(where, total - 1).astype(jnp.int32)
    unroll = next(u for u in (8, 6, 5, 4, 3, 2, 1) if degree_range % u == 0)
    vmem = pl.BlockSpec(memory_space=pltpu.VMEM)
    return pl.pallas_call(
        functools.partial(recurrence_kernel, unroll),
        out_shape=jax.ShapeDtypeStruct((total, slots, latitude_count), jnp.bfloat16),
        in_specs=[pl.BlockSpec(memory_space=pltpu.SMEM)] + [vmem] * 5,
        out_specs=vmem,
        cost_estimate=pl.CostEstimate(
            flops=6 * degree_range * slots * latitude_count,
            bytes_accessed=24 * 1024 * 1024,
            transcendentals=0,
        ),
        name="legendre",
    )(
        where,
        upper,
        lower,
        jnp.broadcast_to(orders[:, None], (slots, LANES)),
        jnp.broadcast_to(cosine, (slots, latitude_count)),
        start,
    )


def quadrature(latitude_count):
    angles = jnp.pi * (jnp.arange(latitude_count).astype(jnp.float32) + 0.5) / latitude_count
    return jnp.pi / latitude_count * jnp.sin(angles)


def exchange(value):
    return lax.all_to_all(value, "order", split_axis=0, concat_axis=0, tiled=True)


def pack(packer, value):
    return jnp.einsum(
        "tpks,tksc->tpc", packer, value, preferred_element_type=jnp.float32
    ).astype(jnp.bfloat16)


def final_kernel(others, table_ref, value_ref, quad_ref, *refs):
    earlier, out_ref = refs[:others], refs[others]
    batch, _, count = table_ref.shape
    for i in range(batch):
        values = value_ref[i].reshape(count, value_ref.shape[-1])
        summed = jnp.dot(table_ref[i], values, preferred_element_type=jnp.float32)
        parts = [ref[i].astype(jnp.float32) for ref in earlier] + [summed * quad_ref[...]]
        out_ref[i] = jnp.stack(parts, axis=1).astype(jnp.bfloat16)


def final_rows(table, values, quad, earlier):
    slots, latitude_count, count = table.shape
    peers, padded, width = values.shape[1:]
    batch = min(4, slots)
    parts = len(earlier) + 1
    return pl.pallas_call(
        functools.partial(final_kernel, len(earlier)),
        grid=(-(-slots // batch),),
        in_specs=[
            pl.BlockSpec((batch, latitude_count, count), lambda i: (i, 0, 0)),
            pl.BlockSpec((batch, peers, padded, width), lambda i: (i, 0, 0, 0)),
            pl.BlockSpec(quad.shape, lambda i: (0, 0)),
        ]
        + [pl.BlockSpec((batch, latitude_count, width), lambda i: (i, 0, 0))] * len(earlier),
        out_specs=pl.BlockSpec((batch, latitude_count, parts, width), lambda i: (i, 0, 0, 0)),
        out_shape=jax.ShapeDtypeStruct((slots, latitude_count, parts, width), jnp.bfloat16),
        compiler_params=pltpu.CompilerParams(vmem_limit_bytes=VMEM_LIMIT),
        cost_estimate=pl.CostEstimate(
            flops=2 * table.size * width,
            bytes_accessed=2 * (table.size + values.size + 2 * parts * slots * latitude_count * width),
            transcendentals=0,
        ),
        name="final",
    )(table, values, quad, *earlier)


def swap(value, bit):
    count = lax.axis_size("chan")
    return lax.ppermute(value, "chan", [(i, i ^ bit) for i in range(count)])


def gather_channels(value):
    count = lax.axis_size("chan")
    if count & (count - 1):
        whole = lax.all_gather(value, "chan", axis=0)
        return [whole[i] for i in range(count)], jnp.arange(count).astype(jnp.int32)
    blocks, flips = [value], [0]
    bit = count // 2
    while bit:
        blocks = blocks + [swap(block, bit) for block in blocks]
        flips = flips + [flip ^ bit for flip in flips]
        bit //= 2
    owners = jnp.bitwise_xor(lax.axis_index("chan"), jnp.array(flips, jnp.int32))
    return blocks, owners


def window_rows(plan_ref, peers, step, window):
    base = step * peers * 3
    spans = []
    for p in range(peers):
        where = pl.multiple_of(plan_ref[base + 3 * p], 16)
        spans.append((pl.ds(where, window), plan_ref[base + 3 * p + 1], plan_ref[base + 3 * p + 2]))
    return spans


def coefficient_kernel(peers, window, blocks, plan_ref, owner_ref, *refs):
    gathered, (weight_ref, out_ref) = refs[:blocks], refs[blocks:]
    step = pl.program_id(0)
    width = out_ref.shape[2]

    @pl.when(step == 0)
    def _():
        out_ref[...] = jnp.zeros_like(out_ref)

    spans = window_rows(plan_ref, peers, step, window)
    total = None
    for b, ref in enumerate(gathered):
        rows = jnp.concatenate([ref[p, span, :] for p, (span, _, _) in enumerate(spans)], axis=0)
        lanes = pl.ds(pl.multiple_of(owner_ref[b] * width, width), width)
        part = lax.dot_general(
            rows, weight_ref[0, :, lanes], (((1,), (1,)), ((), ())), preferred_element_type=jnp.float32
        )
        total = part if total is None else total + part
    index = lax.broadcasted_iota(jnp.int32, (window, width), 0)
    for p, (span, first, _) in enumerate(spans):
        kept = out_ref[p, span, :].astype(jnp.float32)
        fresh = total[p * window : (p + 1) * window]
        out_ref[p, span, :] = jnp.where(index >= first, fresh, kept).astype(jnp.bfloat16)


def mixing_kernel(peers, window, blocks, rows_of, plan_ref, owner_ref, *refs):
    gathered = [refs[r * blocks : (r + 1) * blocks] for r in range(rows_of)]
    saved = refs[rows_of * blocks : rows_of * (blocks + 1)]
    out_ref = refs[-1]
    step = pl.program_id(0)
    width = saved[0].shape[2]
    spans = window_rows(plan_ref, peers, step, window)
    index = lax.broadcasted_iota(jnp.int32, (window, width), 0)
    masked = []
    for r in range(rows_of):
        for p, (span, first, last) in enumerate(spans):
            value = saved[r][p, span, :].astype(jnp.float32)
            inside = (index >= first) & (index < last)
            masked.append(jnp.where(inside, value, 0.0).astype(jnp.bfloat16))
    left = jnp.concatenate(masked, axis=0)
    for b in range(blocks):
        right = jnp.concatenate(
            [gathered[r][b][p, span, :] for r in range(rows_of) for p, (span, _, _) in enumerate(spans)],
            axis=0,
        )
        lanes = pl.ds(pl.multiple_of(owner_ref[b] * width, width), width)
        out_ref[0, :, lanes] = lax.dot_general(
            left, right, (((0,), (0,)), ((), ())), preferred_element_type=jnp.float32
        ).astype(jnp.bfloat16)


def whole_block(shape):
    return pl.BlockSpec(shape, lambda k, *_: (0,) * len(shape), pipeline_mode=pl.Buffered(1))


def coefficients(plan, owners, window, gathered, weights):
    slots, width, channels = weights.shape
    peers = gathered[0].shape[0]
    kernel = functools.partial(coefficient_kernel, peers, window, len(gathered))
    return pl.pallas_call(
        kernel,
        grid_spec=pltpu.PrefetchScalarGridSpec(
            num_scalar_prefetch=2,
            grid=(slots,),
            in_specs=[whole_block(part.shape) for part in gathered]
            + [pl.BlockSpec((1, width, channels), lambda k, *_: (k, 0, 0))],
            out_specs=whole_block(gathered[0].shape),
        ),
        out_shape=jax.ShapeDtypeStruct(gathered[0].shape, jnp.bfloat16),
        compiler_params=pltpu.CompilerParams(vmem_limit_bytes=VMEM_LIMIT),
        cost_estimate=pl.CostEstimate(
            flops=2 * slots * peers * window * width * channels,
            bytes_accessed=2 * (weights.size + (len(gathered) + 1) * gathered[0].size),
            transcendentals=0,
        ),
        name="coefficients",
    )(plan, owners, *gathered, weights)


def mixing_gradients(plan, owners, window, gathered, saved, slots):
    rows_of, blocks = len(gathered), len(gathered[0])
    peers, _, width = saved[0].shape
    operands = [part for parts in gathered for part in parts] + list(saved)
    return pl.pallas_call(
        functools.partial(mixing_kernel, peers, window, blocks, rows_of),
        grid_spec=pltpu.PrefetchScalarGridSpec(
            num_scalar_prefetch=2,
            grid=(slots,),
            in_specs=[whole_block(part.shape) for part in operands],
            out_specs=pl.BlockSpec((1, width, width * blocks), lambda k, *_: (k, 0, 0)),
        ),
        out_shape=jax.ShapeDtypeStruct((slots, width, width * blocks), jnp.bfloat16),
        compiler_params=pltpu.CompilerParams(vmem_limit_bytes=VMEM_LIMIT),
        cost_estimate=pl.CostEstimate(
            flops=2 * slots * peers * window * rows_of * width * width * blocks,
            bytes_accessed=2 * (slots * width * width * blocks + len(operands) * saved[0].size),
            transcendentals=0,
        ),
        name="mixing",
    )(plan, owners, *operands)


def layer(capacity, *operands):
    return layer_body(capacity, *operands)


def layer_body(
    capacity, cotangent, stored_coefficients, weights, order_table, degree_table, mine
):
    slots, latitude_count, batch_size, parts, width = cotangent.shape
    degree_range = stored_coefficients.shape[1]
    peers = lax.axis_size("order")
    full = slots * slots
    rows = batch_size * parts
    cot = cotangent.reshape(slots, latitude_count, rows, width)
    stored = stored_coefficients.reshape(slots, degree_range, rows, width)
    degrees = jnp.arange(degree_range).astype(jnp.int32)

    valid = (degree_table[:, None] >= mine[None, :]) & (degree_table[:, None] < degree_range)
    flags = valid.reshape(peers, full).astype(jnp.bfloat16)
    index = jnp.arange(full)
    before = (index[:, None] < index[None, :]).astype(jnp.bfloat16)
    rank = jnp.dot(flags, before, preferred_element_type=jnp.float32).astype(jnp.int32)
    rank = jnp.where(valid.reshape(peers, full), rank, -1).reshape(peers, slots, slots)
    place = jnp.arange(capacity).astype(jnp.int32)[None, :, None, None]
    packer = (rank[:, None] == place).astype(jnp.bfloat16)

    padded = -(-slots // 16) * 16
    spare = padded - slots
    wide = jnp.pad(rank, ((0, 0), (0, spare), (0, 0)), constant_values=-1)
    wide_packer = (wide[:, None] == place).astype(jnp.bfloat16)

    window = min(-(-slots // 16) * 16 + 16, capacity)
    owned = lax.dynamic_slice_in_dim(degree_table, lax.axis_index("order") * slots, slots)
    lengths = jnp.sum(
        (
            (order_table.reshape(peers, slots)[None] <= owned[:, None, None])
            & (owned[:, None, None] < degree_range)
        ).astype(jnp.int32),
        axis=2,
    )
    steps = jnp.arange(slots)
    earlier = (steps[:, None] > steps[None, :]).astype(jnp.int32)
    offsets = jnp.sum(earlier[:, :, None] * lengths[None], axis=1)
    starts = jnp.minimum(offsets // 16 * 16, capacity - window)
    first = offsets - starts
    plan = jnp.stack([starts, first, first + lengths], axis=2).reshape(-1).astype(jnp.int32)

    pick = (degree_table[:, None, None] == degrees[None, None, :]) & valid[:, :, None]
    pick = pick.astype(jnp.bfloat16).reshape(peers, slots, slots, degree_range)

    def project(matrix, source):
        return jnp.einsum(
            "tksj,sjc->tksc", matrix, source, preferred_element_type=jnp.float32
        ).astype(jnp.bfloat16)

    def send_saved(r):
        return exchange(pack(packer, project(pick, stored[:, :, r])))

    def send_adjoint(r):
        moved = exchange(pack(packer, project(table, cot[:, :, r])))
        return gather_channels(moved)

    saved = [send_saved(0)]
    table = picked_legendre(mine, degree_table, degree_range, latitude_count)
    table = table.reshape(peers, slots, slots, latitude_count)
    turned = jnp.pad(table, ((0, 0), (0, spare), (0, 0), (0, 0))).transpose(2, 3, 0, 1)
    turned = turned.reshape(slots, latitude_count, peers * padded)
    spread = jnp.broadcast_to(quadrature(latitude_count)[:, None], (latitude_count, width))
    gathered = []
    for r in range(rows):
        blocks, owners = send_adjoint(r)
        gathered.append(blocks)
    saved += [send_saved(r) for r in range(1, rows)]
    quad = quadrature(latitude_count)
    outputs = []
    for r in range(rows):
        coefficient = coefficients(plan, owners, window, gathered[r], weights)
        moved = exchange(coefficient)
        form = "tpks,tpc->tksc" if r < rows - 1 else "tpks,tpc->stkc"
        returned = jnp.einsum(
            form,
            packer if r < rows - 1 else wide_packer,
            moved,
            preferred_element_type=jnp.float32,
        ).astype(jnp.bfloat16)
        if r < rows - 1:
            summed = jnp.einsum(
                "tksj,tksc->sjc", table, returned, preferred_element_type=jnp.float32
            )
            outputs.append((summed * quad[None, :, None]).astype(jnp.bfloat16))
        else:
            outputs = final_rows(turned, returned, spread, outputs)
    mixing_gradient = mixing_gradients(plan, owners, window, gathered, saved, slots)
    return outputs.reshape(cotangent.shape), mixing_gradient


def capacities(slots, peers, degree_range):
    full = slots * slots
    live = degree_range * (degree_range + 1) / 2 / (peers * slots) ** 2
    spread = (full * (2 * slots + 1) / 12) ** 0.5
    most = -(-full // 16) * 16
    steps = [-(-int(live * full + s * spread) // 16) * 16 for s in SPREADS]
    return [c for c in steps if c <= 0.85 * most] + [most]


def choose(tier, tiers, operands):
    first = functools.partial(layer, tiers[0])
    if len(tiers) == 1:
        return first(*operands)
    return lax.cond(tier == 0, first, lambda *rest: choose(tier - 1, tiers[1:], rest), *operands)


def per_device(cotangent, stored_coefficients, weights, order_table, degree_table):
    slots = cotangent.shape[0]
    degree_range = stored_coefficients.shape[1]
    peers = lax.axis_size("order")
    position = lax.axis_index("order")
    mine = lax.dynamic_slice_in_dim(order_table, position * slots, slots)
    operands = (cotangent, stored_coefficients, weights, order_table, degree_table, mine)
    tiers = capacities(slots, peers, degree_range)
    if len(tiers) == 1:
        return layer_body(tiers[0], *operands)
    order_rows = order_table.reshape(peers, 1, slots, 1)
    degree_rows = degree_table.reshape(1, peers, 1, slots)
    counts = jnp.sum(
        ((degree_rows >= order_rows) & (degree_rows < degree_range)).astype(jnp.int32), axis=(2, 3)
    )
    most = jnp.max(counts)
    tier = sum((most > c).astype(jnp.int32) for c in tiers[:-1])
    return choose(tier, tiers, operands)


def solution(mesh):
    return jax.shard_map(
        per_device,
        mesh=mesh,
        in_specs=(
            P("order", None, None, None, "chan"),
            P("order", None, None, None, "chan"),
            P("order", "chan", None),
            P(),
            P(),
        ),
        out_specs=(P("order", None, None, None, "chan"), P("order", "chan", None)),
        check_vma=False,
    )
```

```python
import functools

import jax
import jax.numpy as jnp
from jax import lax
from jax.experimental import pallas as pl
from jax.experimental.pallas import tpu as pltpu
from jax.sharding import PartitionSpec as P


SPREADS = (2.1, 2.8, 3.5)
VMEM_LIMIT = 60 * 1024 * 1024
LANES = 128


def recurrence_kernel(unroll, where_ref, upper_ref, lower_ref, order_ref, cosine_ref, start_ref, out_ref):
    degree_range = upper_ref.shape[0]
    latitude_count = out_ref.shape[2]
    pieces = [(lo, min(lo + LANES, latitude_count)) for lo in range(0, latitude_count, LANES)]
    out_ref[...] = jnp.zeros_like(out_ref)
    order = order_ref[...]
    cosine = [cosine_ref[:, lo:hi] for lo, hi in pieces]
    start = [start_ref[:, lo:hi] for lo, hi in pieces]

    def body(step, carry):
        latest, before = carry
        for inner in range(unroll):
            level = step * unroll + inner
            row = where_ref[level]
            upper = upper_ref[level]
            lower = lower_ref[level]
            begins = order == level
            fresh = []
            for i, (lo, hi) in enumerate(pieces):
                width = hi - lo
                grown = upper[:, :width] * (cosine[i] * latest[i] - lower[:, :width] * before[i])
                value = jnp.where(begins[:, :width], start[i], grown)
                out_ref[row, :, lo:hi] = value.astype(jnp.bfloat16)
                fresh.append(value)
            latest, before = fresh, latest
        return latest, before

    zeros = [jnp.zeros_like(c) for c in cosine]
    lax.fori_loop(0, degree_range // unroll, body, (zeros, zeros))


def picked_legendre(orders, degree_table, degree_range, latitude_count):
    slots = orders.shape[0]
    total = degree_table.shape[0]
    order_real = orders.astype(jnp.float32)[:, None]
    angles = jnp.pi * (jnp.arange(latitude_count).astype(jnp.float32) + 0.5) / latitude_count
    cosine = jnp.cos(angles)[None, :]
    sine = jnp.sin(angles)[None, :]
    counter = jnp.arange(1, degree_range + 1).astype(jnp.float32)
    factors = jnp.log((2.0 * counter - 1.0) / (2.0 * counter))
    below = (counter[None, :] <= order_real).astype(jnp.float32)
    log_start = 0.5 * (
        jnp.log((2.0 * order_real + 1.0) / (4.0 * jnp.pi))
        + jnp.sum(below * factors[None, :], axis=1, keepdims=True)
    )
    parity = 1.0 - 2.0 * (orders % 2).astype(jnp.float32)[:, None]
    start = parity * jnp.exp(log_start + order_real * jnp.log(sine))

    level = jnp.arange(degree_range).astype(jnp.float32)[:, None]
    order_wide = order_real[:, 0][None, :]
    upper = jnp.sqrt(
        jnp.maximum(4.0 * level * level - 1.0, 0.0)
        / jnp.maximum(level * level - order_wide * order_wide, 1.0)
    )
    lower = jnp.sqrt(
        jnp.maximum((level - 1.0) * (level - 1.0) - order_wide * order_wide, 0.0)
        / jnp.maximum(4.0 * (level - 1.0) * (level - 1.0) - 1.0, 1.0)
    )
    upper, lower = (
        jnp.broadcast_to(lax.optimization_barrier(part)[:, :, None], part.shape + (LANES,))
        for part in (upper, lower)
    )
    places = jnp.arange(total).astype(jnp.int32)
    degrees = jnp.arange(degree_range).astype(jnp.int32)
    where = jnp.sum(
        jnp.where(degree_table[None, :] == degrees[:, None], places[None, :], 0), axis=1
    )
    where = jnp.minimum(where, total - 1).astype(jnp.int32)
    unroll = next(u for u in (8, 6, 5, 4, 3, 2, 1) if degree_range % u == 0)
    vmem = pl.BlockSpec(memory_space=pltpu.VMEM)
    return pl.pallas_call(
        functools.partial(recurrence_kernel, unroll),
        out_shape=jax.ShapeDtypeStruct((total, slots, latitude_count), jnp.bfloat16),
        in_specs=[pl.BlockSpec(memory_space=pltpu.SMEM)] + [vmem] * 5,
        out_specs=vmem,
        cost_estimate=pl.CostEstimate(
            flops=6 * degree_range * slots * latitude_count,
            bytes_accessed=24 * 1024 * 1024,
            transcendentals=0,
        ),
        name="legendre",
    )(
        where,
        upper,
        lower,
        jnp.broadcast_to(orders[:, None], (slots, LANES)),
        jnp.broadcast_to(cosine, (slots, latitude_count)),
        start,
    )


def quadrature(latitude_count):
    angles = jnp.pi * (jnp.arange(latitude_count).astype(jnp.float32) + 0.5) / latitude_count
    return jnp.pi / latitude_count * jnp.sin(angles)


def exchange(value):
    return lax.all_to_all(value, "order", split_axis=0, concat_axis=0, tiled=True)


def pack(packer, value):
    return jnp.einsum(
        "tpks,tksc->tpc", packer, value, preferred_element_type=jnp.float32
    ).astype(jnp.bfloat16)


def final_kernel(others, table_ref, value_ref, quad_ref, *refs):
    earlier, out_ref = refs[:others], refs[others]
    batch, _, count = table_ref.shape
    for i in range(batch):
        values = value_ref[i].reshape(count, value_ref.shape[-1])
        summed = jnp.dot(table_ref[i], values, preferred_element_type=jnp.float32)
        for r, ref in enumerate(earlier):
            out_ref[i, :, r, :] = ref[i]
        out_ref[i, :, others, :] = (summed * quad_ref[...]).astype(jnp.bfloat16)


def final_rows(table, values, quad, earlier):
    slots, latitude_count, count = table.shape
    peers, padded, width = values.shape[1:]
    batch = min(4, slots)
    parts = len(earlier) + 1
    return pl.pallas_call(
        functools.partial(final_kernel, len(earlier)),
        grid=(-(-slots // batch),),
        in_specs=[
            pl.BlockSpec((batch, latitude_count, count), lambda i: (i, 0, 0)),
            pl.BlockSpec((batch, peers, padded, width), lambda i: (i, 0, 0, 0)),
            pl.BlockSpec(quad.shape, lambda i: (0, 0)),
        ]
        + [pl.BlockSpec((batch, latitude_count, width), lambda i: (i, 0, 0))] * len(earlier),
        out_specs=pl.BlockSpec((batch, latitude_count, parts, width), lambda i: (i, 0, 0, 0)),
        out_shape=jax.ShapeDtypeStruct((slots, latitude_count, parts, width), jnp.bfloat16),
        compiler_params=pltpu.CompilerParams(vmem_limit_bytes=VMEM_LIMIT),
        cost_estimate=pl.CostEstimate(
            flops=2 * table.size * width,
            bytes_accessed=2 * (table.size + values.size + 2 * parts * slots * latitude_count * width),
            transcendentals=0,
        ),
        name="final",
    )(table, values, quad, *earlier)


def swap(value, bit):
    count = lax.axis_size("chan")
    return lax.ppermute(value, "chan", [(i, i ^ bit) for i in range(count)])


def gather_channels(value):
    count = lax.axis_size("chan")
    if count & (count - 1):
        whole = lax.all_gather(value, "chan", axis=0)
        return [whole[i] for i in range(count)], jnp.arange(count).astype(jnp.int32)
    blocks, flips = [value], [0]
    bit = count // 2
    while bit:
        blocks = blocks + [swap(block, bit) for block in blocks]
        flips = flips + [flip ^ bit for flip in flips]
        bit //= 2
    owners = jnp.bitwise_xor(lax.axis_index("chan"), jnp.array(flips, jnp.int32))
    return blocks, owners


def window_rows(plan_ref, peers, step, window):
    base = step * peers * 3
    spans = []
    for p in range(peers):
        where = pl.multiple_of(plan_ref[base + 3 * p], 16)
        spans.append((pl.ds(where, window), plan_ref[base + 3 * p + 1], plan_ref[base + 3 * p + 2]))
    return spans


def coefficient_kernel(peers, window, blocks, plan_ref, owner_ref, *refs):
    gathered, (weight_ref, out_ref) = refs[:blocks], refs[blocks:]
    step = pl.program_id(0)
    width = out_ref.shape[2]

    @pl.when(step == 0)
    def _():
        out_ref[...] = jnp.zeros_like(out_ref)

    spans = window_rows(plan_ref, peers, step, window)
    total = None
    for b, ref in enumerate(gathered):
        rows = jnp.concatenate([ref[p, span, :] for p, (span, _, _) in enumerate(spans)], axis=0)
        lanes = pl.ds(pl.multiple_of(owner_ref[b] * width, width), width)
        part = lax.dot_general(
            rows, weight_ref[0, :, lanes], (((1,), (1,)), ((), ())), preferred_element_type=jnp.float32
        )
        total = part if total is None else total + part
    index = lax.broadcasted_iota(jnp.int32, (window, width), 0)
    for p, (span, first, _) in enumerate(spans):
        kept = out_ref[p, span, :].astype(jnp.float32)
        fresh = total[p * window : (p + 1) * window]
        out_ref[p, span, :] = jnp.where(index >= first, fresh, kept).astype(jnp.bfloat16)


def mixing_kernel(peers, window, blocks, rows_of, plan_ref, owner_ref, *refs):
    gathered = [refs[r * blocks : (r + 1) * blocks] for r in range(rows_of)]
    saved = refs[rows_of * blocks : rows_of * (blocks + 1)]
    out_ref = refs[-1]
    step = pl.program_id(0)
    width = saved[0].shape[2]
    spans = window_rows(plan_ref, peers, step, window)
    index = lax.broadcasted_iota(jnp.int32, (window, width), 0)
    masked = []
    for r in range(rows_of):
        for p, (span, first, last) in enumerate(spans):
            value = saved[r][p, span, :].astype(jnp.float32)
            inside = (index >= first) & (index < last)
            masked.append(jnp.where(inside, value, 0.0).astype(jnp.bfloat16))
    left = jnp.concatenate(masked, axis=0)
    for b in range(blocks):
        right = jnp.concatenate(
            [gathered[r][b][p, span, :] for r in range(rows_of) for p, (span, _, _) in enumerate(spans)],
            axis=0,
        )
        lanes = pl.ds(pl.multiple_of(owner_ref[b] * width, width), width)
        out_ref[0, :, lanes] = lax.dot_general(
            left, right, (((0,), (0,)), ((), ())), preferred_element_type=jnp.float32
        ).astype(jnp.bfloat16)


def whole_block(shape):
    return pl.BlockSpec(shape, lambda k, *_: (0,) * len(shape), pipeline_mode=pl.Buffered(1))


def coefficients(plan, owners, window, gathered, weights):
    slots, width, channels = weights.shape
    peers = gathered[0].shape[0]
    kernel = functools.partial(coefficient_kernel, peers, window, len(gathered))
    return pl.pallas_call(
        kernel,
        grid_spec=pltpu.PrefetchScalarGridSpec(
            num_scalar_prefetch=2,
            grid=(slots,),
            in_specs=[whole_block(part.shape) for part in gathered]
            + [pl.BlockSpec((1, width, channels), lambda k, *_: (k, 0, 0))],
            out_specs=whole_block(gathered[0].shape),
        ),
        out_shape=jax.ShapeDtypeStruct(gathered[0].shape, jnp.bfloat16),
        compiler_params=pltpu.CompilerParams(vmem_limit_bytes=VMEM_LIMIT),
        cost_estimate=pl.CostEstimate(
            flops=2 * slots * peers * window * width * channels,
            bytes_accessed=2 * (weights.size + (len(gathered) + 1) * gathered[0].size),
            transcendentals=0,
        ),
        name="coefficients",
    )(plan, owners, *gathered, weights)


def mixing_gradients(plan, owners, window, gathered, saved, slots):
    rows_of, blocks = len(gathered), len(gathered[0])
    peers, _, width = saved[0].shape
    operands = [part for parts in gathered for part in parts] + list(saved)
    return pl.pallas_call(
        functools.partial(mixing_kernel, peers, window, blocks, rows_of),
        grid_spec=pltpu.PrefetchScalarGridSpec(
            num_scalar_prefetch=2,
            grid=(slots,),
            in_specs=[whole_block(part.shape) for part in operands],
            out_specs=pl.BlockSpec((1, width, width * blocks), lambda k, *_: (k, 0, 0)),
        ),
        out_shape=jax.ShapeDtypeStruct((slots, width, width * blocks), jnp.bfloat16),
        compiler_params=pltpu.CompilerParams(vmem_limit_bytes=VMEM_LIMIT),
        cost_estimate=pl.CostEstimate(
            flops=2 * slots * peers * window * rows_of * width * width * blocks,
            bytes_accessed=2 * (slots * width * width * blocks + len(operands) * saved[0].size),
            transcendentals=0,
        ),
        name="mixing",
    )(plan, owners, *operands)


def layer(capacity, *operands):
    return layer_body(capacity, *operands)


def layer_body(
    capacity, cotangent, stored_coefficients, weights, order_table, degree_table, mine
):
    slots, latitude_count, batch_size, parts, width = cotangent.shape
    degree_range = stored_coefficients.shape[1]
    peers = lax.axis_size("order")
    full = slots * slots
    rows = batch_size * parts
    cot = cotangent.reshape(slots, latitude_count, rows, width)
    stored = stored_coefficients.reshape(slots, degree_range, rows, width)
    degrees = jnp.arange(degree_range).astype(jnp.int32)

    valid = (degree_table[:, None] >= mine[None, :]) & (degree_table[:, None] < degree_range)
    flags = valid.reshape(peers, full).astype(jnp.bfloat16)
    index = jnp.arange(full)
    before = (index[:, None] < index[None, :]).astype(jnp.bfloat16)
    rank = jnp.dot(flags, before, preferred_element_type=jnp.float32).astype(jnp.int32)
    rank = jnp.where(valid.reshape(peers, full), rank, -1).reshape(peers, slots, slots)
    place = jnp.arange(capacity).astype(jnp.int32)[None, :, None, None]
    packer = (rank[:, None] == place).astype(jnp.bfloat16)

    padded = -(-slots // 16) * 16
    spare = padded - slots
    wide = jnp.pad(rank, ((0, 0), (0, spare), (0, 0)), constant_values=-1)
    wide_packer = (wide[:, None] == place).astype(jnp.bfloat16)

    window = min(-(-slots // 16) * 16 + 16, capacity)
    owned = lax.dynamic_slice_in_dim(degree_table, lax.axis_index("order") * slots, slots)
    lengths = jnp.sum(
        (
            (order_table.reshape(peers, slots)[None] <= owned[:, None, None])
            & (owned[:, None, None] < degree_range)
        ).astype(jnp.int32),
        axis=2,
    )
    steps = jnp.arange(slots)
    earlier = (steps[:, None] > steps[None, :]).astype(jnp.int32)
    offsets = jnp.sum(earlier[:, :, None] * lengths[None], axis=1)
    starts = jnp.minimum(offsets // 16 * 16, capacity - window)
    first = offsets - starts
    plan = jnp.stack([starts, first, first + lengths], axis=2).reshape(-1).astype(jnp.int32)

    pick = (degree_table[:, None, None] == degrees[None, None, :]) & valid[:, :, None]
    pick = pick.astype(jnp.bfloat16).reshape(peers, slots, slots, degree_range)

    def project(matrix, source):
        return jnp.einsum(
            "tksj,sjc->tksc", matrix, source, preferred_element_type=jnp.float32
        ).astype(jnp.bfloat16)

    def send_saved(r):
        return exchange(pack(packer, project(pick, stored[:, :, r])))

    def send_adjoint(r):
        moved = exchange(pack(packer, project(table, cot[:, :, r])))
        return gather_channels(moved)

    saved = [send_saved(0)]
    table = picked_legendre(mine, degree_table, degree_range, latitude_count)
    table = table.reshape(peers, slots, slots, latitude_count)
    turned = jnp.pad(table, ((0, 0), (0, spare), (0, 0), (0, 0))).transpose(2, 3, 0, 1)
    turned = turned.reshape(slots, latitude_count, peers * padded)
    spread = jnp.broadcast_to(quadrature(latitude_count)[:, None], (latitude_count, width))
    gathered = []
    for r in range(rows):
        blocks, owners = send_adjoint(r)
        gathered.append(blocks)
    saved += [send_saved(r) for r in range(1, rows)]
    quad = quadrature(latitude_count)
    outputs = []
    for r in range(rows):
        coefficient = coefficients(plan, owners, window, gathered[r], weights)
        moved = exchange(coefficient)
        form = "tpks,tpc->tksc" if r < rows - 1 else "tpks,tpc->stkc"
        returned = jnp.einsum(
            form,
            packer if r < rows - 1 else wide_packer,
            moved,
            preferred_element_type=jnp.float32,
        ).astype(jnp.bfloat16)
        if r < rows - 1:
            summed = jnp.einsum(
                "tksj,tksc->sjc", table, returned, preferred_element_type=jnp.float32
            )
            outputs.append((summed * quad[None, :, None]).astype(jnp.bfloat16))
        else:
            outputs = final_rows(turned, returned, spread, outputs)
    mixing_gradient = mixing_gradients(plan, owners, window, gathered, saved, slots)
    return outputs.reshape(cotangent.shape), mixing_gradient


def capacities(slots, peers, degree_range):
    full = slots * slots
    live = degree_range * (degree_range + 1) / 2 / (peers * slots) ** 2
    spread = (full * (2 * slots + 1) / 12) ** 0.5
    most = -(-full // 16) * 16
    steps = [-(-int(live * full + s * spread) // 16) * 16 for s in SPREADS]
    return [c for c in steps if c <= 0.85 * most] + [most]


def choose(tier, tiers, operands):
    first = functools.partial(layer, tiers[0])
    if len(tiers) == 1:
        return first(*operands)
    return lax.cond(tier == 0, first, lambda *rest: choose(tier - 1, tiers[1:], rest), *operands)


def per_device(cotangent, stored_coefficients, weights, order_table, degree_table):
    slots = cotangent.shape[0]
    degree_range = stored_coefficients.shape[1]
    peers = lax.axis_size("order")
    position = lax.axis_index("order")
    mine = lax.dynamic_slice_in_dim(order_table, position * slots, slots)
    operands = (cotangent, stored_coefficients, weights, order_table, degree_table, mine)
    tiers = capacities(slots, peers, degree_range)
    if len(tiers) == 1:
        return layer_body(tiers[0], *operands)
    order_rows = order_table.reshape(peers, 1, slots, 1)
    degree_rows = degree_table.reshape(1, peers, 1, slots)
    counts = jnp.sum(
        ((degree_rows >= order_rows) & (degree_rows < degree_range)).astype(jnp.int32), axis=(2, 3)
    )
    most = jnp.max(counts)
    tier = sum((most > c).astype(jnp.int32) for c in tiers[:-1])
    return choose(tier, tiers, operands)


def solution(mesh):
    return jax.shard_map(
        per_device,
        mesh=mesh,
        in_specs=(
            P("order", None, None, None, "chan"),
            P("order", None, None, None, "chan"),
            P("order", "chan", None),
            P(),
            P(),
        ),
        out_specs=(P("order", None, None, None, "chan"), P("order", "chan", None)),
        check_vma=False,
    )
```
